256 devices in a mesh: gy: 32 (over z, y), gx: 8 (over x, core).
Axes of the slice: x: 4, y: 4, z: 8, core: 2. Of those that a mesh axis runs over, the one named last changes fastest.
Arguments:
- bins: int32 [4, 512, 8192], P(None, 'gy', 'gx'), may hold values from 0 to 4095
- mask: int32 [4, 512, 8192], P(None, 'gy', 'gx'), may hold values from 0 to 1
- atlas: bfloat16 [8, 4, 512, 8192], P(None, None, 'gy', 'gx'), may hold values from -100 to 130
- init_mean: float32 [8], replicated, may hold values from 0.05 to 0.95
- init_scale: float32 [8], replicated, may hold values from 0.004 to 0.15
Outputs:
- phase_prob: bfloat16 [8, 4, 512, 8192], P(None, None, 'gy', 'gx')
- em_params: float32 [3, 8], replicated
- bin_density: float32 [4096], P(('gy', 'gx'))
The draws below stay inside these ranges and needn't reach their ends.
All inputs are finite; a program needn't handle non-finite values.
Results may differ from the reference program's by a relative error of at most 0.0015.
Values may be sent and summed in bfloat16 or wider, within the bound.
A program may use at most 64 MiB of HBM per device.

```python
import jax
import jax.numpy as jnp
from jax import lax

PH = 8
NB = 4096
EM_ITERS = 5
POTTS = 3
Z = 4
ROWS_DEV = 16
COLS_DEV = 1024
NY = 512
NX = 8192


def tile_field(table):
    return jnp.repeat(jnp.repeat(table, ROWS_DEV, axis=0), COLS_DEV, axis=1)


def draw_bins(key, part):
    tiles_y = NY // ROWS_DEV
    tiles_x = NX // COLS_DEV
    shape = (Z, NY, NX)
    phase = jax.random.randint(jax.random.fold_in(key, 1), shape, 0, PH)
    tile_phase = tile_field(jax.random.randint(jax.random.fold_in(key, 2), (tiles_y, tiles_x), 0, PH))
    pick = jax.random.randint(jax.random.fold_in(key, 3), shape, 0, 2)
    phase = jnp.where(pick == 1, tile_phase[None], phase)
    center = (2 * phase + 1) * NB // (2 * PH)
    noise = jnp.zeros(shape, jnp.int32)
    for index in range(4):
        noise = noise + jax.random.randint(jax.random.fold_in(key, 10 + index), shape, -(NB // 20), NB // 20 + 1)
    shift = tile_field(jax.random.randint(jax.random.fold_in(key, 4), (tiles_y, tiles_x), -(NB // 32), NB // 32 + 1))
    return jnp.clip(center + noise + shift[None], 0, NB - 1).astype(jnp.int32)


def draw_mask(key, part):
    tiles_y = NY // ROWS_DEV
    tiles_x = NX // COLS_DEV
    rank = jnp.arange(tiles_y, dtype=jnp.int32)[:, None] * jnp.ones((1, tiles_x), jnp.int32)
    level = 200 + 600 * rank // max(tiles_y - 1, 1)
    level = level + jax.random.randint(jax.random.fold_in(key, 1), (tiles_y, tiles_x), -50, 51)
    level = tile_field(level)
    roll = jax.random.randint(jax.random.fold_in(key, 2), (Z, NY, NX), 0, 1000)
    return (roll < level[None]).astype(jnp.int32)


def draw_atlas(key, part):
    shape = (PH, Z, NY, NX)
    values = 1.5 * jax.random.normal(jax.random.fold_in(key, 1), shape, jnp.float32)
    return values.astype(jnp.bfloat16)


def draw_init_scale(key, part):
    low, high = (0.03, 0.15)
    unit = jax.random.uniform(jax.random.fold_in(key, 1), (PH,), jnp.float32)
    return jnp.exp(jnp.log(low) + unit * (jnp.log(high) - jnp.log(low))).astype(jnp.float32)


def setup_inputs(seed: int = 0) -> dict:
    key_of = jax.random.split(jax.random.key(seed), 6)
    return {
        "bins": draw_bins(jax.random.fold_in(key_of[5], 71), 0),
        "mask": draw_mask(jax.random.fold_in(key_of[5], 71), 0),
        "atlas": draw_atlas(jax.random.fold_in(key_of[5], 71), 0),
        "init_mean": jnp.clip(jax.random.uniform(key_of[3], (PH,), jnp.float32, 0.05, 0.95), 0.05, 0.95),
        "init_scale": draw_init_scale(jax.random.fold_in(key_of[5], 71), 0),
    }


VAR_EPS = 1e-5
BETA = 0.3


def phase_scores(values, mean, var, weight):
    shape = (mean.shape[0],) + (1,) * values.ndim
    m = mean.reshape(shape)
    v = var.reshape(shape)
    w = weight.reshape(shape)
    diff = values[None] - m
    return (jnp.log(w) - 0.5 * jnp.log(v)) - diff * diff / (2.0 * v)


def moments(counts, centers, mean, var, weight):
    resp = jax.nn.softmax(phase_scores(centers, mean, var, weight), axis=0)
    weighted = resp * counts[None]
    return jnp.stack([jnp.sum(weighted, 1), jnp.sum(weighted * centers[None], 1),
                      jnp.sum(weighted * (centers * centers)[None], 1)])


def refit(sums, count_phases):
    occ, first, second = sums[0], sums[1], sums[2]
    mean = first / (occ + 1.0)
    var = (second - first * mean) / (occ + 1.0) + VAR_EPS
    weight = (occ + 1.0) / (jnp.sum(occ) + count_phases)
    return mean, var, weight


def cycle_plane(padded, rows, cols):
    total = jnp.zeros((padded.shape[0], rows, cols), jnp.float32)
    for dy in range(-2, 3):
        for dx in range(-2, 3):
            if dy != 0 or dx != 0:
                piece = padded[:, 2 + dy:2 + dy + rows, 2 + dx:2 + dx + cols].astype(jnp.float32)
                total = total + piece * (1.0 / (dy * dy + dx * dx))
    return total


def reference(bins, mask, atlas, init_mean, init_scale):
    counts = jax.ops.segment_sum(mask.reshape(-1).astype(jnp.float32), bins.reshape(-1), num_segments=NB)
    planes, rows, cols = bins.shape
    density = counts * (float(NB) / float(planes * rows * cols))
    centers = (jnp.arange(NB, dtype=jnp.int32).astype(jnp.float32) + 0.5) / NB
    mean = init_mean
    var = init_scale * init_scale
    weight = jnp.full((PH,), 1.0 / PH, jnp.float32)
    for step in range(EM_ITERS):
        mean, var, weight = refit(moments(counts, centers, mean, var, weight), float(PH))
    params = jnp.stack([mean, var, weight])
    fg = mask.astype(jnp.float32)

    def unary_plane(z):
        plane_bins = lax.dynamic_index_in_dim(bins, z, 0, keepdims=False)
        values = (plane_bins.astype(jnp.float32) + 0.5) / NB
        plane_atlas = lax.dynamic_index_in_dim(atlas, z, 1, keepdims=False).astype(jnp.float32)
        return phase_scores(values, mean, var, weight) + plane_atlas

    zidx = jnp.arange(planes, dtype=jnp.int32)
    q = lax.map(lambda z: jax.nn.softmax(unary_plane(z), axis=0).astype(jnp.bfloat16), zidx)
    q = jnp.transpose(q, (1, 0, 2, 3))
    for step in range(POTTS):
        held = (q.astype(jnp.float32) * fg[None]).astype(jnp.bfloat16)

        def update(z):
            own = lax.dynamic_index_in_dim(held, z, 1, keepdims=False)
            padded = jnp.pad(own, ((0, 0), (2, 2), (2, 2)))
            cycle = cycle_plane(padded, rows, cols)
            lower = lax.dynamic_index_in_dim(held, jnp.maximum(z - 1, 0), 1, keepdims=False).astype(jnp.float32)
            upper = lax.dynamic_index_in_dim(held, jnp.minimum(z + 1, planes - 1), 1, keepdims=False).astype(jnp.float32)
            lower = lower * (z > 0).astype(jnp.float32)
            upper = upper * (z < planes - 1).astype(jnp.float32)
            field = cycle + (lower + upper)
            return jax.nn.softmax(unary_plane(z) + BETA * field, axis=0).astype(jnp.bfloat16)

        q = jnp.transpose(lax.map(update, zidx), (1, 0, 2, 3))
    phase_prob = (q.astype(jnp.float32) * fg[None]).astype(jnp.bfloat16)
    return (phase_prob, params, density)
```

```python
import math

import jax
import jax.numpy as jnp
from jax import lax
from jax.sharding import PartitionSpec as P

NB = 4096
EM_ITERS = 5
POTTS = 3


VAR_EPS = 1e-05
BETA = 0.3


def extended(x, sides, width):
    for axis, dim in sides:
        size, length = (lax.axis_size(axis), x.shape[dim])
        up = [(i, (i + 1) % size) for i in range(size - 1)]
        down = [(j, i) for i, j in up]
        last = lax.slice_in_dim(x, length - width, length, axis=dim)
        initial = lax.slice_in_dim(x, 0, width, axis=dim)
        before = lax.ppermute(last, axis, up)
        after = lax.ppermute(initial, axis, down)
        x = jnp.concatenate([before, x, after], axis=dim)
    return x


def phase_scores(values, mean, var, weight):
    shape = (mean.shape[0],) + (1,) * values.ndim
    m = mean.reshape(shape)
    v = var.reshape(shape)
    w = weight.reshape(shape)
    diff = values[None] - m
    return jnp.log(w) - 0.5 * jnp.log(v) - diff * diff / (2.0 * v)


def moments(counts, centers, mean, var, weight):
    resp = jax.nn.softmax(phase_scores(centers, mean, var, weight), axis=0)
    weighted = resp * counts[None]
    return jnp.stack(
        [
            jnp.sum(weighted, 1),
            jnp.sum(weighted * centers[None], 1),
            jnp.sum(weighted * (centers * centers)[None], 1),
        ]
    )


def refit(sums, count_phases):
    occ, first, second = (sums[0], sums[1], sums[2])
    mean = first / (occ + 1.0)
    var = (second - first * mean) / (occ + 1.0) + VAR_EPS
    weight = (occ + 1.0) / (jnp.sum(occ) + count_phases)
    return (mean, var, weight)


def cycle_total(padded, rows, cols):
    total = jnp.zeros(padded.shape[:2] + (rows, cols), jnp.float32)
    for dy in range(-2, 3):
        for dx in range(-2, 3):
            if dy != 0 or dx != 0:
                piece = padded[:, :, 2 + dy : 2 + dy + rows, 2 + dx : 2 + dx + cols].astype(
                    jnp.float32
                )
                total = total + piece * (1.0 / (dy * dy + dx * dx))
    return total


def plane_total(held):
    padded = jnp.pad(held.astype(jnp.float32), ((0, 0), (1, 1), (0, 0), (0, 0)))
    return padded[:, :-2] + padded[:, 2:]


def per_device(bins, mask, atlas, init_mean, init_scale):
    planes, rows, cols = bins.shape
    phases = init_mean.shape[0]
    devices_all = lax.axis_size("gy") * lax.axis_size("gx")
    scale_factor = float(NB) / float(planes * rows * cols * devices_all)
    group = math.gcd(16, planes * rows)
    block_bins = bins.reshape(-1, group * cols)
    block_mask = mask.reshape(-1, group * cols)
    high_count = NB // 128

    def count_block(acc, item):
        part_bins, part_mask = item
        high = part_bins // 128
        low = part_bins % 128
        high_hot = (high[None, :] == jnp.arange(high_count, dtype=jnp.int32)[:, None]).astype(
            jnp.bfloat16
        )
        high_hot = high_hot * part_mask.astype(jnp.bfloat16)[None, :]
        low_hot = (low[None, :] == jnp.arange(128, dtype=jnp.int32)[:, None]).astype(jnp.bfloat16)
        table = lax.dot_general(
            high_hot, low_hot, (((1,), (1,)), ((), ())), preferred_element_type=jnp.float32
        )
        return (acc + table, None)

    table, _ = lax.scan(
        count_block, jnp.zeros((high_count, 128), jnp.float32), (block_bins, block_mask)
    )
    counts = table.reshape(NB)
    mean = init_mean
    var = init_scale * init_scale
    weight = jnp.full((phases,), 1.0 / phases, jnp.float32)
    counts = lax.psum(counts, ("gy", "gx"))
    part = NB // devices_all
    start = lax.axis_index(("gy", "gx")) * part
    density = lax.dynamic_slice_in_dim(counts, start, part) * scale_factor
    centers = (jnp.arange(NB, dtype=jnp.int32).astype(jnp.float32) + 0.5) / NB
    for step in range(EM_ITERS):
        sums = moments(counts, centers, mean, var, weight)
        mean, var, weight = refit(sums, float(phases))
    params = jnp.stack([mean, var, weight])
    intensity = (bins.astype(jnp.float32) + 0.5) / NB
    unary = phase_scores(intensity, mean, var, weight) + atlas.astype(jnp.float32)
    fg = mask.astype(jnp.float32)
    q = jax.nn.softmax(unary, axis=0).astype(jnp.bfloat16)
    for step in range(POTTS):
        held = (q.astype(jnp.float32) * fg[None]).astype(jnp.bfloat16)
        padded = extended(held, (("gy", 2), ("gx", 3)), 2)
        field = cycle_total(padded, rows, cols) + plane_total(held)
        q = jax.nn.softmax(unary + BETA * field, axis=0).astype(jnp.bfloat16)
    phase_prob = (q.astype(jnp.float32) * fg[None]).astype(jnp.bfloat16)
    return (phase_prob, params, density)


def solution(mesh):
    in_specs = (P(None, "gy", "gx"), P(None, "gy", "gx"), P(None, None, "gy", "gx"), P(), P())
    out_specs = (P(None, None, "gy", "gx"), P(), P(("gy", "gx")))
    return jax.shard_map(
        per_device, mesh=mesh, in_specs=in_specs, out_specs=out_specs, check_vma=False
    )
```

```python
import functools
import math

import jax
import jax.numpy as jnp
import numpy as np
from jax import lax
from jax.experimental import pallas as pl
from jax.experimental.pallas import tpu as pltpu
from jax.sharding import PartitionSpec as P

NB = 4096
EM_ITERS = 5
VAR_EPS = 1e-05
BETA = 0.3
LOG2E = math.log2(math.e)
MESH = pl.DeviceIdType.MESH

PH = 8
PL = 4
ROWS = 16
COLS = 1024
STEP = 116
CHUNKS = 9
NX, NY, NZ = 4, 4, 8


def neighbours(gy, gx, ny, nx):
    up, down = lax.rem(gy + ny - 1, ny), lax.rem(gy + 1, ny)
    left, right = lax.rem(gx + nx - 1, nx), lax.rem(gx + 1, nx)
    return up, down, left, right


def front_kernel(
    bins_ref, mask_ref, atlas_ref,
    counts_ref, rows_a, side_a, corner_a, rows_c, side_c, corner_c,
    code, high, low, half, core_in, x_in, y_in, z_in, stage, total,
    halo_send, halo_recv, sum_send, sum_recv,
):
    ny, nx = lax.axis_size("gy"), lax.axis_size("gx")
    gy, gx = lax.axis_index("gy"), lax.axis_index("gx")
    up, down, left, right = neighbours(gy, gx, ny, nx)
    core, x = lax.rem(gx, 2), gx // 2
    y, z = lax.rem(gy, NY), gy // NY
    other = gx + 1 - 2 * core
    along_x = [(gy, lax.rem(x + d, NX) * 2 + core) for d in range(1, NX)]
    along_y = [(z * NY + lax.rem(y + d, NY), gx) for d in range(1, NY)]
    along_z = [(lax.rem(z + d, NZ) * NY + y, gx) for d in range(1, NZ)]
    around = [
        (up, gx), (down, gx), (gy, left), (gy, right),
        (up, left), (up, right), (down, left), (down, right),
    ]
    partners = [(gy, other)] + along_x + along_y + along_z + around

    barrier = pltpu.get_barrier_semaphore()
    for device in partners:
        pl.semaphore_signal(barrier, inc=1, device_id=device, device_id_type=MESH)

    code[...] = bins_ref[...] + NB * mask_ref[...]
    for plane in range(PL):
        b = bins_ref[plane]
        keep = mask_ref[plane] > 0
        high[plane * ROWS : (plane + 1) * ROWS, :] = jnp.where(keep, b // 64, 255).astype(jnp.float32)
        low[plane * ROWS : (plane + 1) * ROWS, :] = (b & 63).astype(jnp.float32)

    pl.semaphore_wait(barrier, len(partners))

    bottom, top = pl.ds(ROWS - 8, 8), pl.ds(0, 8)
    last, first = pl.ds(COLS - 128, 128), pl.ds(0, 128)
    every, wide = pl.ds(0, ROWS), pl.ds(0, COLS)
    plan = [
        ((up, gx), top, wide, rows_a.at[1], rows_c.at[1]),
        ((down, gx), bottom, wide, rows_a.at[0], rows_c.at[0]),
        ((gy, left), every, first, side_a.at[1], side_c.at[1]),
        ((gy, right), every, last, side_a.at[0], side_c.at[0]),
        ((up, left), top, first, corner_a.at[3], corner_c.at[3]),
        ((up, right), top, last, corner_a.at[2], corner_c.at[2]),
        ((down, left), bottom, first, corner_a.at[1], corner_c.at[1]),
        ((down, right), bottom, last, corner_a.at[0], corner_c.at[0]),
    ]
    copies = []
    for n, (device, r, c, to_a, to_c) in enumerate(plan):
        for m, (src, dst) in enumerate(((atlas_ref.at[:, :, r, c], to_a), (code.at[:, r, c], to_c))):
            copies.append(
                pltpu.make_async_remote_copy(
                    src_ref=src, dst_ref=dst,
                    send_sem=halo_send.at[2 * n + m], recv_sem=halo_recv.at[2 * n + m],
                    device_id=device, device_id_type=MESH,
                )
            )
    for copy in copies:
        copy.start()

    levels = lax.broadcasted_iota(jnp.int32, (64, COLS), 0).astype(jnp.float32).astype(jnp.bfloat16)
    one, zero = jnp.ones((), jnp.bfloat16), jnp.zeros((), jnp.bfloat16)
    total[...] = jnp.zeros_like(total)

    def count(r, carry):
        h = jnp.broadcast_to(high[pl.ds(r, 1), :], (64, COLS)).astype(jnp.bfloat16)
        l = jnp.broadcast_to(low[pl.ds(r, 1), :], (64, COLS)).astype(jnp.bfloat16)
        hot_h = jnp.where(h == levels, one, zero)
        hot_l = jnp.where(l == levels, one, zero)
        total[...] += lax.dot_general(
            hot_h, hot_l, (((1,), (1,)), ((), ())), preferred_element_type=jnp.float32
        )
        return carry

    lax.fori_loop(0, PL * ROWS, count, 0)
    mine = total[...]
    half[...] = mine

    def exchange(src, dst, device, n):
        return pltpu.make_async_remote_copy(
            src_ref=src, dst_ref=dst, send_sem=sum_send.at[n], recv_sem=sum_recv.at[n],
            device_id=device, device_id_type=MESH,
        )

    keep_rows = pl.ds(pl.multiple_of(core * 32, 32), 32)
    give_rows = pl.ds(pl.multiple_of((1 - core) * 32, 32), 32)
    done = []
    copy = exchange(half.at[give_rows], core_in, (gy, other), 0)
    copy.start()
    copy.wait_recv()
    done.append(copy)
    stage[0] = half[keep_rows, :] + core_in[...]
    n = 1
    for level, (group, landing) in enumerate(((along_x, x_in), (along_y, y_in), (along_z, z_in))):
        now = []
        for i, device in enumerate(group):
            now.append(exchange(stage.at[level], landing.at[i], device, n))
            n += 1
        for copy in now:
            copy.start()
        acc = stage[level]
        for i, copy in enumerate(now):
            copy.wait_recv()
            acc = acc + landing[i]
        stage[level + 1] = acc
        done += now
    copy = exchange(stage.at[3], counts_ref.at[keep_rows], (gy, other), n)
    copy.start()
    counts_ref[keep_rows, :] = stage[3]
    copy.wait_recv()
    done.append(copy)
    for copy in done:
        copy.wait_send()
    for copy in copies:
        copy.wait()


def front(bins, mask, atlas):
    f32, bf16, i32 = jnp.float32, jnp.bfloat16, jnp.int32
    vmem = pl.BlockSpec(memory_space=pltpu.VMEM)
    anywhere = pl.BlockSpec(memory_space=pl.ANY)
    sds = jax.ShapeDtypeStruct
    sums = 2 + (NX - 1) + (NY - 1) + (NZ - 1)
    return pl.pallas_call(
        front_kernel,
        out_shape=(
            sds((64, 64), f32),
            sds((2, PH, PL, 8, COLS), bf16),
            sds((2, PH, PL, ROWS, 128), bf16),
            sds((4, PH, PL, 8, 128), bf16),
            sds((2, PL, 8, COLS), i32),
            sds((2, PL, ROWS, 128), i32),
            sds((4, PL, 8, 128), i32),
        ),
        in_specs=[vmem, vmem, anywhere],
        out_specs=(vmem,) + (anywhere,) * 6,
        scratch_shapes=[
            pltpu.VMEM((PL, ROWS, COLS), i32),
            pltpu.VMEM((PL * ROWS, COLS), f32),
            pltpu.VMEM((PL * ROWS, COLS), f32),
            pltpu.VMEM((64, 64), f32),
            pltpu.VMEM((32, 64), f32),
            pltpu.VMEM((NX - 1, 32, 64), f32),
            pltpu.VMEM((NY - 1, 32, 64), f32),
            pltpu.VMEM((NZ - 1, 32, 64), f32),
            pltpu.VMEM((4, 32, 64), f32),
            pltpu.VMEM((64, 64), f32),
            pltpu.SemaphoreType.DMA((16,)),
            pltpu.SemaphoreType.DMA((16,)),
            pltpu.SemaphoreType.DMA((sums,)),
            pltpu.SemaphoreType.DMA((sums,)),
        ],
        compiler_params=pltpu.CompilerParams(collective_id=0, has_side_effects=True),
        name="histogram_and_halo",
    )(bins, mask, atlas)


def fit(counts_ref, mean, scale):
    wide = [jnp.broadcast_to(counts_ref[r : r + 1, :], (PH, 128)) for r in range(NB // 128)]
    counts = jnp.concatenate(wide, axis=1)
    centers = (lax.broadcasted_iota(jnp.int32, (PH, NB), 1).astype(jnp.float32) + 0.5) / NB
    first_w = counts * centers
    second_w = first_w * centers
    var = scale * scale
    weight = jnp.full((PH, 1), 1.0 / PH, jnp.float32)
    for step in range(EM_ITERS):
        diff = centers - mean
        scores = (jnp.log(weight) - 0.5 * jnp.log(var)) - diff * diff * (0.5 / var)
        e = jnp.exp(scores - jnp.max(scores, axis=0, keepdims=True))
        resp = e * (1.0 / jnp.sum(e, axis=0, keepdims=True))
        occ = jnp.sum(resp * counts, axis=1, keepdims=True)
        first = jnp.sum(resp * first_w, axis=1, keepdims=True)
        second = jnp.sum(resp * second_w, axis=1, keepdims=True)
        mean = first / (occ + 1.0)
        var = (second - first * mean) / (occ + 1.0) + VAR_EPS
        weight = (occ + 1.0) / (jnp.sum(occ, axis=0, keepdims=True) + float(PH))
    return mean, var, weight


def softmax_into(t, r_mask):
    top = functools.reduce(jnp.maximum, t)
    e = [jnp.exp2(v - top) for v in t]
    inv = jnp.where(r_mask > 0.0, 1.0 / functools.reduce(jnp.add, e), 0.0)
    return [v * inv for v in e]


def back_kernel(
    place_ref, counts_ref, mean_ref, scale_ref, bins_ref, mask_ref, atlas_ref,
    rows_a, side_a, corner_a, rows_c, side_c, corner_c, w_ref,
    prob_ref, params_ref, density_ref,
    apad, cpad, coef, uns, msk, held, held24, pa, pb, pd, ps, kept,
):
    f32, bf16 = jnp.float32, jnp.bfloat16
    gy, gx = place_ref[0], place_ref[1]
    ny, nx = place_ref[2], place_ref[3]

    row = counts_ref[pl.ds(gy, 1), :] * place_scale(bins_ref)
    density_ref[...] = pltpu.roll(jnp.broadcast_to(row, (8, 128)), lax.rem(128 - gx * 16, 128), 1)[0:1, 0:16]
    mean, var, weight = fit(counts_ref, mean_ref[...], scale_ref[...])
    lane = lax.broadcasted_iota(jnp.int32, (PH, 128), 1)
    diag = lane == lax.broadcasted_iota(jnp.int32, (PH, 128), 0)
    for n, column in enumerate((mean, var, weight)):
        spread = jnp.where(diag, jnp.broadcast_to(column, (PH, 128)), 0.0)
        params_ref[n : n + 1, :] = jnp.sum(spread, axis=0, keepdims=True)[:, 0:PH]
    offset = (jnp.log(weight) - 0.5 * jnp.log(var)) * LOG2E
    slope = (0.5 * LOG2E) / var
    for n, column in enumerate((mean, offset, slope)):
        full = jnp.broadcast_to(column, (PH, 128))
        for k in range(PH):
            coef[n, k] = jnp.broadcast_to(full[k : k + 1, :], (8, 128))

    own, over = pl.ds(128, COLS), pl.ds(128 + COLS, 128)

    def fill(k, carry):
        for plane in range(PL):
            apad[k, plane, 8:24, own] = atlas_ref[k, plane]
            apad[k, plane, 8:24, 0:128] = side_a[0, k, plane]
            apad[k, plane, 8:24, over] = side_a[1, k, plane]
            apad[k, plane, 0:8, own] = rows_a[0, k, plane]
            apad[k, plane, 24:32, own] = rows_a[1, k, plane]
            apad[k, plane, 0:8, 0:128] = corner_a[0, k, plane]
            apad[k, plane, 0:8, over] = corner_a[1, k, plane]
            apad[k, plane, 24:32, 0:128] = corner_a[2, k, plane]
            apad[k, plane, 24:32, over] = corner_a[3, k, plane]
        return carry

    lax.fori_loop(0, PH, fill, 0)
    has_up, has_down = gy > 0, gy < ny - 1
    has_left, has_right = gx > 0, gx < nx - 1
    cpad[:, 8:24, own] = bins_ref[...] + NB * mask_ref[...]
    cpad[:, 8:24, 0:128] = jnp.where(has_left, side_c[0], 0)
    cpad[:, 8:24, over] = jnp.where(has_right, side_c[1], 0)
    cpad[:, 0:8, own] = jnp.where(has_up, rows_c[0], 0)
    cpad[:, 24:32, own] = jnp.where(has_down, rows_c[1], 0)
    cpad[:, 0:8, 0:128] = jnp.where(has_up & has_left, corner_c[0], 0)
    cpad[:, 0:8, over] = jnp.where(has_up & has_right, corner_c[1], 0)
    cpad[:, 24:32, 0:128] = jnp.where(has_down & has_left, corner_c[2], 0)
    cpad[:, 24:32, over] = jnp.where(has_down & has_right, corner_c[3], 0)

    held[PL] = jnp.zeros_like(held[PL])
    held24[PL] = jnp.zeros_like(held24[PL])
    ps[0] = jnp.zeros_like(ps[0])
    for ref in (pa, pb, pd):
        for plane in range(PL):
            ref[plane, 0:8] = jnp.zeros((8, 128), f32)
            ref[plane, 200:208] = jnp.zeros((8, 128), f32)
    beta = BETA / 5.0 * LOG2E
    at = lax.broadcasted_iota(jnp.int32, (8, 128), 1)

    def spread_sums(src, per, lead):
        def plane_dot(plane, carry):
            both = jnp.concatenate([src[plane], src[plane + 1]], axis=1)
            out = jnp.dot(both, w_ref[...], preferred_element_type=f32)
            span = pl.ds(lead, per)
            pa[plane, span, :] = out[:, 0:128]
            pb[plane, span, :] = out[:, 128:256]
            pd[plane, span, :] = out[:, 256:384]
            ps[plane + 1, span, :] = out[:, 384:512]
            return carry

        lax.fori_loop(0, PL, plane_dot, 0)

    def update(plane, start, u_start, m_start, per):
        t = []
        for k in range(PH):
            r = k * per + start
            total = pa[plane, pl.ds(r, 8), :] + ps[plane, pl.ds(r, 8), :]
            total = total + (pb[plane, pl.ds(r - 1, 8), :] + pb[plane, pl.ds(r + 1, 8), :])
            total = total + (pd[plane, pl.ds(r - 2, 8), :] + pd[plane, pl.ds(r + 2, 8), :])
            t.append(uns[plane, pl.ds(k * 32 + u_start, 8), :] + beta * total)
        return softmax_into(t, msk[plane, pl.ds(m_start, 8), :])

    def chunk(c, carry):
        turn = 12 * c + 6
        from_right = at < 128 - turn - 0

        def moved(a, b):
            return pltpu.roll(jnp.where(from_right, b, a), turn, 1)

        tile_a = pl.ds(pl.multiple_of(c * 128, 128), 128)
        tile_b = pl.ds(pl.multiple_of((c + 1) * 128, 128), 128)

        def begin(plane, carry):
            for pair in range(2):
                outs = []
                rows16 = pl.ds(pair * 16, 16)
                left = [apad[k, plane, rows16, tile_a].astype(f32) for k in range(PH)]
                right = [apad[k, plane, rows16, tile_b].astype(f32) for k in range(PH)]
                for sub in range(2):
                    g = pair * 16 + sub * 8
                    s8 = slice(sub * 8, sub * 8 + 8)
                    cd = moved(cpad[plane, pl.ds(g, 8), tile_a], cpad[plane, pl.ds(g, 8), tile_b])
                    keep = cd >= NB
                    m = jnp.where(keep, 1.0, 0.0)
                    msk[plane, pl.ds(g, 8), :] = m
                    s = ((cd & (NB - 1)).astype(f32) + 0.5) * (1.0 / NB)
                    t = []
                    for k in range(PH):
                        prior = moved(left[k][s8], right[k][s8])
                        d = s - coef[0, k]
                        u = (coef[1, k] - d * d * coef[2, k]) + prior * LOG2E
                        u = jnp.where(keep, u, 0.0)
                        uns[plane, pl.ds(k * 32 + g, 8), :] = u
                        t.append(u)
                    outs.append(softmax_into(t, m))
                for k in range(PH):
                    both = jnp.concatenate([outs[0][k], outs[1][k]], axis=0)
                    held[plane, pl.ds(k * 32 + pair * 16, 16), :] = both.astype(bf16)
            return carry

        lax.fori_loop(0, PL, begin, 0)

        def store24(plane, outs):
            flat = [outs[i][k] for k in range(PH) for i in range(3)]
            for f in range(0, 3 * PH, 2):
                both = jnp.concatenate([flat[f], flat[f + 1]], axis=0)
                held24[plane, pl.ds(f * 8, 16), :] = both.astype(bf16)

        spread_sums(held, 256, 0)

        def second(plane, carry):
            store24(plane, [update(plane, 4 + 8 * i, 4 + 8 * i, 4 + 8 * i, 32) for i in range(3)])
            return carry

        lax.fori_loop(0, PL, second, 0)
        spread_sums(held24, 192, 8)

        def third(plane, carry):
            store24(plane, [update(plane, 8 + 8 * i, 4 + 8 * i, 4 + 8 * i, 24) for i in range(3)])
            return carry

        lax.fori_loop(0, PL, third, 0)
        spread_sums(held24, 192, 8)
        slot = lax.rem(c, 2)
        before = at < STEP + 12 - 12 * c
        tile_out = pl.ds(pl.multiple_of(jnp.maximum(c - 1, 0) * 128, 128), 128)

        def last(plane, carry):
            outs = [update(plane, 8 + 4 + 8 * i, 8 + 8 * i, 8 + 8 * i, 24) for i in range(2)]
            for k in range(PH):
                full = []
                for i in range(2):
                    v = pltpu.roll(outs[i][k], 128 - turn, 1)
                    old = kept[1 - slot, plane, k, pl.ds(8 * i, 8), :]
                    kept[slot, plane, k, pl.ds(8 * i, 8), :] = v
                    full.append(jnp.where(before, old, v))
                prob_ref[k, plane, :, tile_out] = jnp.concatenate(full, axis=0).astype(bf16)
            return carry

        lax.fori_loop(0, PL, last, 0)
        return carry

    lax.fori_loop(0, CHUNKS, chunk, 0)


def place_scale(bins_ref):
    planes, rows, cols = bins_ref.shape
    return float(NB) / float(planes * rows * cols * 2 * NX * NY * NZ)


def stencil_weights():
    i = np.arange(128)
    d = np.abs(i[:, None] - i[None, :])

    def band(*values):
        out = np.zeros((128, 128), np.float32)
        for n, v in enumerate(values):
            out[d == n] = v
        return out

    eye, none = band(5.0), np.zeros((128, 128), np.float32)
    own = np.concatenate([band(0.0, 5.0, 1.25), band(5.0, 2.5, 1.0), band(1.25, 1.0, 0.625), eye], 1)
    above = np.concatenate([eye, none, none, none], 1)
    return np.concatenate([own, above], 0)


def back(place, counts, mean, scale, bins, mask, atlas, halos):
    f32, bf16, i32 = jnp.float32, jnp.bfloat16, jnp.int32
    vmem = pl.BlockSpec(memory_space=pltpu.VMEM)
    sds = jax.ShapeDtypeStruct
    weights = jnp.asarray(stencil_weights(), bf16)
    return pl.pallas_call(
        back_kernel,
        out_shape=(sds((PH, PL, ROWS, COLS), bf16), sds((3, PH), f32), sds((1, 16), f32)),
        in_specs=[pl.BlockSpec(memory_space=pltpu.SMEM)] + [vmem] * 13,
        out_specs=(vmem, vmem, vmem),
        scratch_shapes=[
            pltpu.VMEM((PH, PL, 32, COLS + 256), bf16),
            pltpu.VMEM((PL, 32, COLS + 256), i32),
            pltpu.VMEM((3, PH, 8, 128), f32),
            pltpu.VMEM((PL, PH * 32, 128), f32),
            pltpu.VMEM((PL, 32, 128), f32),
            pltpu.VMEM((PL + 1, PH * 32, 128), bf16),
            pltpu.VMEM((PL + 1, PH * 24, 128), bf16),
            pltpu.VMEM((PL, PH * 32, 128), f32),
            pltpu.VMEM((PL, PH * 32, 128), f32),
            pltpu.VMEM((PL, PH * 32, 128), f32),
            pltpu.VMEM((PL + 1, PH * 32, 128), f32),
            pltpu.VMEM((2, PL, PH, ROWS, 128), f32),
        ],
        name="fit_and_label",
    )(place, counts, mean, scale, bins, mask, atlas, *halos, weights)


def per_device(bins, mask, atlas, init_mean, init_scale):
    counts, *halos = front(bins, mask, atlas)
    place = jnp.stack(
        [lax.axis_index("gy"), lax.axis_index("gx"), lax.axis_size("gy"), lax.axis_size("gx")]
    ).astype(jnp.int32)
    prob, params, density = back(
        place, counts.reshape(NB // 128, 128), init_mean[:, None], init_scale[:, None], bins, mask, atlas, halos
    )
    return prob, params, density.reshape(-1)


def solution(mesh):
    in_specs = (P(None, "gy", "gx"), P(None, "gy", "gx"), P(None, None, "gy", "gx"), P(), P())
    out_specs = (P(None, None, "gy", "gx"), P(), P(("gy", "gx")))
    return jax.shard_map(
        per_device, mesh=mesh, in_specs=in_specs, out_specs=out_specs, check_vma=False
    )
```

```python
import functools
import math

import jax
import jax.numpy as jnp
import numpy as np
from jax import lax
from jax.experimental import pallas as pl
from jax.experimental.pallas import tpu as pltpu
from jax.sharding import PartitionSpec as P

NB = 4096
EM_ITERS = 5
VAR_EPS = 1e-05
BETA = 0.3
LOG2E = math.log2(math.e)
MESH = pl.DeviceIdType.MESH

PH = 8
PL = 4
ROWS = 16
COLS = 1024
STEP = 116
CHUNKS = 9
NX, NY, NZ = 4, 4, 8


def neighbours(gy, gx, ny, nx):
    up, down = lax.rem(gy + ny - 1, ny), lax.rem(gy + 1, ny)
    left, right = lax.rem(gx + nx - 1, nx), lax.rem(gx + 1, nx)
    return up, down, left, right


def front_kernel(
    bins_ref, mask_ref, atlas_ref,
    counts_ref, rows_a, side_a, corner_a, rows_c, side_c, corner_c,
    code, high, low, half, core_in, x_in, y_in, z_in, stage, total,
    halo_send, halo_recv, sum_send, sum_recv,
):
    ny, nx = lax.axis_size("gy"), lax.axis_size("gx")
    gy, gx = lax.axis_index("gy"), lax.axis_index("gx")
    up, down, left, right = neighbours(gy, gx, ny, nx)
    core, x = lax.rem(gx, 2), gx // 2
    y, z = lax.rem(gy, NY), gy // NY
    other = gx + 1 - 2 * core
    along_x = [(gy, lax.rem(x + d, NX) * 2 + core) for d in range(1, NX)]
    along_y = [(z * NY + lax.rem(y + d, NY), gx) for d in range(1, NY)]
    along_z = [(lax.rem(z + d, NZ) * NY + y, gx) for d in range(1, NZ)]
    around = [
        (up, gx), (down, gx), (gy, left), (gy, right),
        (up, left), (up, right), (down, left), (down, right),
    ]
    partners = [(gy, other)] + along_x + along_y + along_z + around

    barrier = pltpu.get_barrier_semaphore()
    for device in partners:
        pl.semaphore_signal(barrier, inc=1, device_id=device, device_id_type=MESH)

    code[...] = bins_ref[...] + NB * mask_ref[...]
    for plane in range(PL):
        b = bins_ref[plane]
        keep = mask_ref[plane] > 0
        high[plane * ROWS : (plane + 1) * ROWS, :] = jnp.where(keep, b // 64, 255).astype(jnp.float32)
        low[plane * ROWS : (plane + 1) * ROWS, :] = (b & 63).astype(jnp.float32)

    levels = lax.broadcasted_iota(jnp.int32, (64, COLS), 0).astype(jnp.float32).astype(jnp.bfloat16)
    one, zero = jnp.ones((), jnp.bfloat16), jnp.zeros((), jnp.bfloat16)
    total[...] = jnp.zeros_like(total)

    def count(step, carry):
        hot = [], []
        for row in range(8):
            for digits, out in zip((high, low), hot):
                wide = jnp.broadcast_to(digits[pl.ds(step * 8 + row, 1), :], (64, COLS))
                out.append(jnp.where(wide.astype(jnp.bfloat16) == levels, one, zero))
        total[...] += lax.dot_general(
            jnp.concatenate(hot[0], axis=1), jnp.concatenate(hot[1], axis=1),
            (((1,), (1,)), ((), ())), preferred_element_type=jnp.float32,
        )
        return carry

    lax.fori_loop(0, PL * ROWS // 16, count, 0)
    pl.semaphore_wait(barrier, len(partners))

    bottom, top = pl.ds(ROWS - 8, 8), pl.ds(0, 8)
    last, first = pl.ds(COLS - 128, 128), pl.ds(0, 128)
    every, wide = pl.ds(0, ROWS), pl.ds(0, COLS)
    plan = [
        ((up, gx), top, wide, rows_a.at[1], rows_c.at[1]),
        ((down, gx), bottom, wide, rows_a.at[0], rows_c.at[0]),
        ((gy, left), every, first, side_a.at[1], side_c.at[1]),
        ((gy, right), every, last, side_a.at[0], side_c.at[0]),
        ((up, left), top, first, corner_a.at[3], corner_c.at[3]),
        ((up, right), top, last, corner_a.at[2], corner_c.at[2]),
        ((down, left), bottom, first, corner_a.at[1], corner_c.at[1]),
        ((down, right), bottom, last, corner_a.at[0], corner_c.at[0]),
    ]
    copies = []
    for n, (device, r, c, to_a, to_c) in enumerate(plan):
        for m, (src, dst) in enumerate(((atlas_ref.at[:, :, r, c], to_a), (code.at[:, r, c], to_c))):
            copies.append(
                pltpu.make_async_remote_copy(
                    src_ref=src, dst_ref=dst,
                    send_sem=halo_send.at[2 * n + m], recv_sem=halo_recv.at[2 * n + m],
                    device_id=device, device_id_type=MESH,
                )
            )
    for copy in copies:
        copy.start()

    lax.fori_loop(PL * ROWS // 16, PL * ROWS // 8, count, 0)
    mine = total[...]
    half[...] = mine

    def exchange(src, dst, device, n):
        return pltpu.make_async_remote_copy(
            src_ref=src, dst_ref=dst, send_sem=sum_send.at[n], recv_sem=sum_recv.at[n],
            device_id=device, device_id_type=MESH,
        )

    keep_rows = pl.ds(pl.multiple_of(core * 32, 32), 32)
    give_rows = pl.ds(pl.multiple_of((1 - core) * 32, 32), 32)
    done = []
    copy = exchange(half.at[give_rows], core_in, (gy, other), 0)
    copy.start()
    copy.wait_recv()
    done.append(copy)
    stage[0] = half[keep_rows, :] + core_in[...]
    n = 1
    for level, (group, landing) in enumerate(((along_x, x_in), (along_y, y_in), (along_z, z_in))):
        now = []
        for i, device in enumerate(group):
            now.append(exchange(stage.at[level], landing.at[i], device, n))
            n += 1
        for copy in now:
            copy.start()
        acc = stage[level]
        for i, copy in enumerate(now):
            copy.wait_recv()
            acc = acc + landing[i]
        stage[level + 1] = acc
        done += now
    copy = exchange(stage.at[3], counts_ref.at[keep_rows], (gy, other), n)
    copy.start()
    counts_ref[keep_rows, :] = stage[3]
    copy.wait_recv()
    done.append(copy)
    for copy in done:
        copy.wait_send()
    for copy in copies:
        copy.wait()


def front(bins, mask, atlas):
    f32, bf16, i32 = jnp.float32, jnp.bfloat16, jnp.int32
    vmem = pl.BlockSpec(memory_space=pltpu.VMEM)
    anywhere = pl.BlockSpec(memory_space=pl.ANY)
    sds = jax.ShapeDtypeStruct
    sums = 2 + (NX - 1) + (NY - 1) + (NZ - 1)
    return pl.pallas_call(
        front_kernel,
        out_shape=(
            sds((64, 64), f32),
            sds((2, PH, PL, 8, COLS), bf16),
            sds((2, PH, PL, ROWS, 128), bf16),
            sds((4, PH, PL, 8, 128), bf16),
            sds((2, PL, 8, COLS), i32),
            sds((2, PL, ROWS, 128), i32),
            sds((4, PL, 8, 128), i32),
        ),
        in_specs=[vmem, vmem, anywhere],
        out_specs=(vmem,) + (anywhere,) * 6,
        scratch_shapes=[
            pltpu.VMEM((PL, ROWS, COLS), i32),
            pltpu.VMEM((PL * ROWS, COLS), f32),
            pltpu.VMEM((PL * ROWS, COLS), f32),
            pltpu.VMEM((64, 64), f32),
            pltpu.VMEM((32, 64), f32),
            pltpu.VMEM((NX - 1, 32, 64), f32),
            pltpu.VMEM((NY - 1, 32, 64), f32),
            pltpu.VMEM((NZ - 1, 32, 64), f32),
            pltpu.VMEM((4, 32, 64), f32),
            pltpu.VMEM((64, 64), f32),
            pltpu.SemaphoreType.DMA((16,)),
            pltpu.SemaphoreType.DMA((16,)),
            pltpu.SemaphoreType.DMA((sums,)),
            pltpu.SemaphoreType.DMA((sums,)),
        ],
        compiler_params=pltpu.CompilerParams(collective_id=0, has_side_effects=True),
        name="histogram_and_halo",
    )(bins, mask, atlas)


def fit(table, mean, scale):
    wide = [jnp.broadcast_to(table[r : r + 1, :], (PH, 128)) for r in range(NB // 128)]
    counts = jnp.concatenate(wide, axis=1)
    at = lax.broadcasted_iota(jnp.int32, (PH, NB), 1)
    bins = 64 * (at // 128) + (at & 63) + NB // 128 * (at & 64)
    centers = (bins.astype(jnp.float32) + 0.5) / NB
    first_w = counts * centers
    second_w = first_w * centers
    var = scale * scale
    weight = jnp.full((PH, 1), 1.0 / PH, jnp.float32)
    for step in range(EM_ITERS):
        diff = centers - mean
        scores = (jnp.log(weight) - 0.5 * jnp.log(var)) - diff * diff * (0.5 / var)
        e = jnp.exp(scores - jnp.max(scores, axis=0, keepdims=True))
        resp = e * (1.0 / jnp.sum(e, axis=0, keepdims=True))
        occ = jnp.sum(resp * counts, axis=1, keepdims=True)
        first = jnp.sum(resp * first_w, axis=1, keepdims=True)
        second = jnp.sum(resp * second_w, axis=1, keepdims=True)
        mean = first / (occ + 1.0)
        var = (second - first * mean) / (occ + 1.0) + VAR_EPS
        weight = (occ + 1.0) / (jnp.sum(occ, axis=0, keepdims=True) + float(PH))
    return mean, var, weight


def total_of(parts, op):
    while len(parts) > 1:
        parts = [op(a, b) for a, b in zip(parts[::2], parts[1::2])]
    return parts[0]


def softmax_into(t, mask):
    e = [jnp.exp2(v) for v in t]
    inv = mask / total_of(e, jnp.add)
    return [v * inv for v in e]


def back_kernel(
    counts_ref, mean_ref, scale_ref, bins_ref, mask_ref, atlas_ref,
    rows_a, side_a, corner_a, rows_c, side_c, corner_c, w_ref,
    prob_ref, params_ref, density_ref,
    table, apad, cpad, coef, uns, msk, held, held24, pa, pb, pd, across, kept,
):
    f32, bf16 = jnp.float32, jnp.bfloat16
    gy, gx = lax.axis_index("gy"), lax.axis_index("gx")
    ny, nx = lax.axis_size("gy"), lax.axis_size("gx")

    table[...] = jnp.concatenate([counts_ref[0:32, :], counts_ref[32:64, :]], axis=1)
    start = 2 * gy + gx // 4
    row = table[pl.ds(lax.rem(start, 32), 1), :] * place_scale(bins_ref)
    skip = start // 32 * 64 + lax.rem(gx, 4) * 16
    density_ref[...] = pltpu.roll(jnp.broadcast_to(row, (8, 128)), lax.rem(128 - skip, 128), 1)[0:1, 0:16]
    phase = lax.broadcasted_iota(jnp.int32, (PH, 1), 0)
    mean, scale = jnp.zeros((PH, 1), f32), jnp.zeros((PH, 1), f32)
    for k in range(PH):
        mean = jnp.where(phase == k, mean_ref[k], mean)
        scale = jnp.where(phase == k, scale_ref[k], scale)
    mean, var, weight = fit(table, mean, scale)
    lane = lax.broadcasted_iota(jnp.int32, (PH, 128), 1)
    diag = lane == lax.broadcasted_iota(jnp.int32, (PH, 128), 0)
    for n, column in enumerate((mean, var, weight)):
        spread = jnp.where(diag, jnp.broadcast_to(column, (PH, 128)), 0.0)
        params_ref[n : n + 1, :] = jnp.sum(spread, axis=0, keepdims=True)[:, 0:PH]
    offset = (jnp.log(weight) - 0.5 * jnp.log(var)) * LOG2E
    slope = (0.5 * LOG2E) / var
    for n, column in enumerate((mean, offset, slope)):
        full = jnp.broadcast_to(column, (PH, 128))
        for k in range(PH):
            coef[n, k] = jnp.broadcast_to(full[k : k + 1, :], (8, 128))

    own, over = pl.ds(128, COLS), pl.ds(128 + COLS, 128)

    def fill(k, carry):
        for plane in range(PL):
            apad[k, plane, 8:24, own] = atlas_ref[k, plane]
            apad[k, plane, 8:24, 0:128] = side_a[0, k, plane]
            apad[k, plane, 8:24, over] = side_a[1, k, plane]
            apad[k, plane, 0:8, own] = rows_a[0, k, plane]
            apad[k, plane, 24:32, own] = rows_a[1, k, plane]
            apad[k, plane, 0:8, 0:128] = corner_a[0, k, plane]
            apad[k, plane, 0:8, over] = corner_a[1, k, plane]
            apad[k, plane, 24:32, 0:128] = corner_a[2, k, plane]
            apad[k, plane, 24:32, over] = corner_a[3, k, plane]
        return carry

    lax.fori_loop(0, PH, fill, 0)
    has_up, has_down = gy > 0, gy < ny - 1
    has_left, has_right = gx > 0, gx < nx - 1
    cpad[:, 8:24, own] = bins_ref[...] + NB * mask_ref[...]
    cpad[:, 8:24, 0:128] = jnp.where(has_left, side_c[0], 0)
    cpad[:, 8:24, over] = jnp.where(has_right, side_c[1], 0)
    cpad[:, 0:8, own] = jnp.where(has_up, rows_c[0], 0)
    cpad[:, 24:32, own] = jnp.where(has_down, rows_c[1], 0)
    cpad[:, 0:8, 0:128] = jnp.where(has_up & has_left, corner_c[0], 0)
    cpad[:, 0:8, over] = jnp.where(has_up & has_right, corner_c[1], 0)
    cpad[:, 24:32, 0:128] = jnp.where(has_down & has_left, corner_c[2], 0)
    cpad[:, 24:32, over] = jnp.where(has_down & has_right, corner_c[3], 0)

    for ref in (pa, pb, pd):
        for plane in range(PL):
            ref[plane, 0:8] = jnp.zeros((8, 128), f32)
            ref[plane, 200:208] = jnp.zeros((8, 128), f32)
    beta = BETA / 5.0 * LOG2E
    at = lax.broadcasted_iota(jnp.int32, (8, 128), 1)

    def spread_sums(src, per, lead, pair):
        both = jnp.concatenate([src[2 * pair], src[2 * pair + 1]], axis=1)
        out = jnp.dot(both, w_ref[...], preferred_element_type=f32)
        span = pl.ds(lead, per)
        for i in range(2):
            for n, ref in enumerate((pa, pb, pd)):
                m = 3 * i + n
                ref[2 * pair + i, span, :] = out[:, 128 * m : 128 * m + 128]

    def update(side, plane, start, u_start, m_start, per):
        t = []
        for k in range(PH):
            r = k * per + start
            total = pa[plane, pl.ds(r, 8), :]
            if plane in (1, 2):
                total = total + across[side, 2 - plane, pl.ds(r, 8), :]
            total = total + (pb[plane, pl.ds(r - 1, 8), :] + pb[plane, pl.ds(r + 1, 8), :])
            total = total + (pd[plane, pl.ds(r - 2, 8), :] + pd[plane, pl.ds(r + 2, 8), :])
            t.append(uns[plane, pl.ds(k * 32 + u_start, 8), :] + beta * total)
        return softmax_into(t, msk[plane, pl.ds(m_start, 8), :])

    def store(side, ref, plane, row, lead, both):
        both = both.astype(bf16)
        ref[plane, pl.ds(row, 16), :] = both
        if plane in (1, 2):
            across[side, plane - 1, pl.ds(row + lead, 16), :] = 5.0 * both.astype(f32)

    def chunk(c, carry):
        turn = 12 * c + 6
        from_right = at < 128 - turn

        def moved(a, b):
            return pltpu.roll(jnp.where(from_right, b, a), turn, 1)

        tile_a = pl.ds(pl.multiple_of(c * 128, 128), 128)
        tile_b = pl.ds(pl.multiple_of((c + 1) * 128, 128), 128)
        wide_right = jnp.concatenate([from_right, from_right], axis=0)

        def begin(plane):
            for pair in range(2):
                outs = []
                rows16 = pl.ds(pair * 16, 16)
                prior = []
                for k in range(PH):
                    one = apad[k, plane, rows16, tile_a].astype(f32)
                    two = apad[k, plane, rows16, tile_b].astype(f32)
                    prior.append(jnp.where(wide_right, two, one))
                for sub in range(2):
                    g = pair * 16 + sub * 8
                    s8 = slice(sub * 8, sub * 8 + 8)
                    cd = moved(cpad[plane, pl.ds(g, 8), tile_a], cpad[plane, pl.ds(g, 8), tile_b])
                    keep = cd >= NB
                    m = jnp.where(keep, 1.0, 0.0)
                    msk[plane, pl.ds(g, 8), :] = m
                    s = ((cd & (NB - 1)).astype(f32) + 0.5) * (1.0 / NB)
                    t = []
                    for k in range(PH):
                        d = s - coef[0, k]
                        u = (coef[1, k] - d * d * coef[2, k]) + pltpu.roll(prior[k][s8], turn, 1) * LOG2E
                        t.append(u)
                    top = total_of(t, jnp.maximum)
                    t = [u - top for u in t]
                    for k in range(PH):
                        uns[plane, pl.ds(k * 32 + g, 8), :] = t[k]
                    outs.append(softmax_into(t, m))
                for k in range(PH):
                    store(0, held, plane, k * 32 + pair * 16, 0, jnp.concatenate([outs[0][k], outs[1][k]], axis=0))

        def store24(side, plane, outs):
            flat = [outs[i][k] for k in range(PH) for i in range(3)]
            for f in range(0, 3 * PH, 2):
                store(side, held24, plane, f * 8, 8, jnp.concatenate([flat[f], flat[f + 1]], axis=0))

        for plane in range(PL):
            begin(plane)
        for pair in range(PL // 2):
            spread_sums(held, 256, 0, pair)
        for plane in range(PL):
            store24(1, plane, [update(0, plane, 4 + 8 * i, 4 + 8 * i, 4 + 8 * i, 32) for i in range(3)])
        for pair in range(PL // 2):
            spread_sums(held24, 192, 8, pair)
        for plane in range(PL):
            store24(0, plane, [update(1, plane, 8 + 8 * i, 4 + 8 * i, 4 + 8 * i, 24) for i in range(3)])
        for pair in range(PL // 2):
            spread_sums(held24, 192, 8, pair)
        slot = lax.rem(c, 2)
        before = at < STEP + 12 - 12 * c
        tile_out = pl.ds(pl.multiple_of(jnp.maximum(c - 1, 0) * 128, 128), 128)
        for plane in range(PL):
            outs = [update(0, plane, 8 + 4 + 8 * i, 8 + 8 * i, 8 + 8 * i, 24) for i in range(2)]
            for k in range(PH):
                full = []
                for i in range(2):
                    v = pltpu.roll(outs[i][k], 128 - turn, 1)
                    old = kept[1 - slot, plane, k, pl.ds(8 * i, 8), :]
                    kept[slot, plane, k, pl.ds(8 * i, 8), :] = v
                    full.append(jnp.where(before, old, v))
                prob_ref[k, plane, :, tile_out] = jnp.concatenate(full, axis=0).astype(bf16)
        return carry

    lax.fori_loop(0, CHUNKS, chunk, 0)


def place_scale(bins_ref):
    planes, rows, cols = bins_ref.shape
    return float(NB) / float(planes * rows * cols * 2 * NX * NY * NZ)


def stencil_weights():
    i = np.arange(128)
    d = np.abs(i[:, None] - i[None, :])

    def band(*values):
        out = np.zeros((128, 128), np.float32)
        for n, v in enumerate(values):
            out[d == n] = v
        return out

    flat, one, two = band(0.0, 5.0, 1.25), band(5.0, 2.5, 1.0), band(1.25, 1.0, 0.625)
    eye, none = band(5.0), np.zeros((128, 128), np.float32)
    upper = np.concatenate([flat, one, two, eye, none, none], 1)
    lower = np.concatenate([eye, none, none, flat, one, two], 1)
    return np.concatenate([upper, lower], 0)


def back(counts, mean, scale, bins, mask, atlas, halos):
    f32, bf16, i32 = jnp.float32, jnp.bfloat16, jnp.int32
    vmem, smem = pl.BlockSpec(memory_space=pltpu.VMEM), pl.BlockSpec(memory_space=pltpu.SMEM)
    sds = jax.ShapeDtypeStruct
    weights = jnp.asarray(stencil_weights(), bf16)
    return pl.pallas_call(
        back_kernel,
        out_shape=(sds((PH, PL, ROWS, COLS), bf16), sds((3, PH), f32), sds((1, 16), f32)),
        in_specs=[vmem, smem, smem] + [vmem] * 10,
        out_specs=(vmem, vmem, vmem),
        scratch_shapes=[
            pltpu.VMEM((NB // 128, 128), f32),
            pltpu.VMEM((PH, PL, 32, COLS + 256), bf16),
            pltpu.VMEM((PL, 32, COLS + 256), i32),
            pltpu.VMEM((3, PH, 8, 128), f32),
            pltpu.VMEM((PL, PH * 32, 128), f32),
            pltpu.VMEM((PL, 32, 128), f32),
            pltpu.VMEM((PL, PH * 32, 128), bf16),
            pltpu.VMEM((PL, PH * 24, 128), bf16),
            pltpu.VMEM((PL, PH * 32, 128), f32),
            pltpu.VMEM((PL, PH * 32, 128), f32),
            pltpu.VMEM((PL, PH * 32, 128), f32),
            pltpu.VMEM((2, 2, PH * 32, 128), f32),
            pltpu.VMEM((2, PL, PH, ROWS, 128), f32),
        ],
        name="fit_and_label",
    )(counts, mean, scale, bins, mask, atlas, *halos, weights)


def per_device(bins, mask, atlas, init_mean, init_scale):
    counts, *halos = front(bins, mask, atlas)
    prob, params, density = back(counts, init_mean, init_scale, bins, mask, atlas, halos)
    return prob, params, density.reshape(-1)


def solution(mesh):
    in_specs = (P(None, "gy", "gx"), P(None, "gy", "gx"), P(None, None, "gy", "gx"), P(), P())
    out_specs = (P(None, None, "gy", "gx"), P(), P(("gy", "gx")))
    return jax.shard_map(
        per_device, mesh=mesh, in_specs=in_specs, out_specs=out_specs, check_vma=False
    )
```

```python
import functools
import math

import jax
import jax.numpy as jnp
import numpy as np
from jax import lax
from jax.experimental import pallas as pl
from jax.experimental.pallas import tpu as pltpu
from jax.sharding import PartitionSpec as P

NB = 4096
EM_ITERS = 5
VAR_EPS = 1e-05
BETA = 0.3
LOG2E = math.log2(math.e)
MESH = pl.DeviceIdType.MESH

PH = 8
PL = 4
ROWS = 16
COLS = 1024
STEP = 116
HALO = 6
SHARE = 3, 1, 2, 4, 0
CHUNKS = 9
NX, NY, NZ = 4, 4, 8


def neighbours(gy, gx, ny, nx):
    up, down = lax.rem(gy + ny - 1, ny), lax.rem(gy + 1, ny)
    left, right = lax.rem(gx + nx - 1, nx), lax.rem(gx + 1, nx)
    return up, down, left, right


def front_kernel(
    bins_ref, mask_ref, atlas_ref,
    counts_ref, rows_a, side_a, corner_a, rows_c, side_c, corner_c,
    code, high, low, edges, strips_a, strips_c, half, core_in, x_in, y_in, z_in, stage, total,
    edge_sem, halo_send, halo_recv, sum_send, sum_recv,
):
    ny, nx = lax.axis_size("gy"), lax.axis_size("gx")
    gy, gx = lax.axis_index("gy"), lax.axis_index("gx")
    up, down, left, right = neighbours(gy, gx, ny, nx)
    core, x = lax.rem(gx, 2), gx // 2
    y, z = lax.rem(gy, NY), gy // NY
    other = gx + 1 - 2 * core
    along_x = [(gy, lax.rem(x + d, NX) * 2 + core) for d in range(1, NX)]
    along_y = [(z * NY + lax.rem(y + d, NY), gx) for d in range(1, NY)]
    along_z = [(lax.rem(z + d, NZ) * NY + y, gx) for d in range(1, NZ)]
    around = [
        (up, gx), (down, gx), (gy, left), (gy, right),
        (up, left), (up, right), (down, left), (down, right),
    ]
    partners = [(gy, other)] + along_x + along_y + along_z + around

    barrier = pltpu.get_barrier_semaphore()
    for device in partners:
        pl.semaphore_signal(barrier, inc=1, device_id=device, device_id_type=MESH)

    edge_copies = [
        pltpu.make_async_copy(atlas_ref.at[:, :, :, pl.ds(lane, 128)], edges.at[n], edge_sem.at[n])
        for n, lane in enumerate((0, COLS - 128))
    ]
    for copy in edge_copies:
        copy.start()
    code[...] = bins_ref[...] + NB * mask_ref[...]
    for plane in range(PL):
        b = bins_ref[plane]
        keep = mask_ref[plane] > 0
        high[plane * ROWS : (plane + 1) * ROWS, :] = jnp.where(keep, b // 64, 255).astype(jnp.float32)
        low[plane * ROWS : (plane + 1) * ROWS, :] = (b & 63).astype(jnp.float32)

    levels = lax.broadcasted_iota(jnp.int32, (64, COLS), 0).astype(jnp.float32).astype(jnp.bfloat16)
    one, zero = jnp.ones((), jnp.bfloat16), jnp.zeros((), jnp.bfloat16)
    total[...] = jnp.zeros_like(total)

    def count(step, carry):
        hot = [], []
        for row in range(8):
            for digits, out in zip((high, low), hot):
                wide = jnp.broadcast_to(digits[pl.ds(step * 8 + row, 1), :], (64, COLS))
                out.append(jnp.where(wide.astype(jnp.bfloat16) == levels, one, zero))
        total[...] += lax.dot_general(
            jnp.concatenate(hot[0], axis=1), jnp.concatenate(hot[1], axis=1),
            (((1,), (1,)), ((), ())), preferred_element_type=jnp.float32,
        )
        return carry

    lax.fori_loop(0, PL * ROWS // 16, count, 0)

    for copy in edge_copies:
        copy.wait()
    place = lax.broadcasted_iota(jnp.int32, (8, 128), 1) // 8
    for n in range(4):
        row, side = 8 * (n // 2), n % 2
        tiles = []
        for tile in range(2):
            acc = jnp.zeros((8, 128), jnp.float32)
            for i in range(16):
                k, plane = divmod(16 * tile + i, PL)
                v = edges[side, k, plane].astype(jnp.float32)[row : row + 8]
                acc = jnp.where(place == i, pltpu.roll(v, (8 * i + 8 * side) % 128, 1), acc)
            tiles.append(acc)
        strips_a[n] = jnp.concatenate(tiles, axis=0).astype(jnp.bfloat16)
        acc = jnp.zeros((8, 128), jnp.int32)
        for plane in range(PL):
            v = code[plane, row : row + 8, (COLS - 128) * side : (COLS - 128) * side + 128]
            acc = jnp.where(place == plane, pltpu.roll(v, 8 * plane + 8 * side, 1), acc)
        strips_c[n] = acc
    pl.semaphore_wait(barrier, len(partners))

    bottom, top = pl.ds(ROWS - HALO, HALO), pl.ds(0, HALO)
    last, first = pl.ds(COLS - 128, 128), pl.ds(0, 128)

    def block(r, c):
        return atlas_ref.at[:, :, r, c], code.at[:, r, c]

    every, wide = pl.ds(0, ROWS), pl.ds(0, COLS)
    plan = []
    for k in range(PH):
        for n, device, r in ((1, (up, gx), top), (0, (down, gx), bottom)):
            plan.append((device, (atlas_ref.at[k, :, r, wide],), (rows_a.at[n, k],)))
    for ps in (pl.ds(0, PL // 2), pl.ds(PL // 2, PL // 2)):
        for n, device, r in ((1, (up, gx), top), (0, (down, gx), bottom)):
            plan.append((device, (code.at[ps, r, wide],), (rows_c.at[n, ps],)))
    pieces = len(plan)
    plan += [
        ((gy, left), block(every, first), (side_a.at[1], side_c.at[1])),
        ((gy, right), block(every, last), (side_a.at[0], side_c.at[0])),
    ]
    diagonal = (up, left), (up, right), (down, left), (down, right)
    for n, device in enumerate(diagonal):
        to = corner_a.at[3 - n], corner_c.at[3 - n]
        plan.append((device, (strips_a.at[n], strips_c.at[n]), to))
    copies = []
    for device, give, take in plan:
        for src, dst in zip(give, take):
            copies.append(
                pltpu.make_async_remote_copy(
                    src_ref=src, dst_ref=dst,
                    send_sem=halo_send.at[len(copies)], recv_sem=halo_recv.at[len(copies)],
                    device_id=device, device_id_type=MESH,
                )
            )
    queue = list(copies[:pieces])

    def send(count):
        for copy in queue[: 2 * count]:
            copy.start()
        del queue[: 2 * count]

    send(SHARE[0])
    for copy in copies[pieces:]:
        copy.start()

    lax.fori_loop(PL * ROWS // 16, PL * ROWS // 8, count, 0)
    mine = total[...]
    half[...] = mine

    def exchange(src, dst, device, n):
        return pltpu.make_async_remote_copy(
            src_ref=src, dst_ref=dst, send_sem=sum_send.at[n], recv_sem=sum_recv.at[n],
            device_id=device, device_id_type=MESH,
        )

    keep_rows = pl.ds(pl.multiple_of(core * 32, 32), 32)
    give_rows = pl.ds(pl.multiple_of((1 - core) * 32, 32), 32)
    done = []
    copy = exchange(half.at[give_rows], core_in, (gy, other), 0)
    copy.start()
    send(SHARE[1])
    copy.wait_recv()
    done.append(copy)
    stage[0] = half[keep_rows, :] + core_in[...]
    n = 1
    for level, (group, landing) in enumerate(((along_x, x_in), (along_z, z_in), (along_y, y_in))):
        now = []
        for i, device in enumerate(group):
            now.append(exchange(stage.at[level], landing.at[i], device, n))
            n += 1
        for copy in now:
            copy.start()
        send(SHARE[2 + level])
        acc = stage[level]
        for i, copy in enumerate(now):
            copy.wait_recv()
            acc = acc + landing[i]
        stage[level + 1] = acc
        done += now
    copy = exchange(stage.at[3], counts_ref.at[keep_rows], (gy, other), n)
    copy.start()
    counts_ref[keep_rows, :] = stage[3]
    copy.wait_recv()
    done.append(copy)
    for copy in done:
        copy.wait_send()
    for copy in copies:
        copy.wait()


def front(bins, mask, atlas):
    f32, bf16, i32 = jnp.float32, jnp.bfloat16, jnp.int32
    vmem = pl.BlockSpec(memory_space=pltpu.VMEM)
    anywhere = pl.BlockSpec(memory_space=pl.ANY)
    sds = jax.ShapeDtypeStruct
    sums = 2 + (NX - 1) + (NY - 1) + (NZ - 1)
    return pl.pallas_call(
        front_kernel,
        out_shape=(
            sds((64, 64), f32),
            sds((2, PH, PL, HALO, COLS), bf16),
            sds((2, PH, PL, ROWS, 128), bf16),
            sds((4, 16, 128), bf16),
            sds((2, PL, HALO, COLS), i32),
            sds((2, PL, ROWS, 128), i32),
            sds((4, 8, 128), i32),
        ),
        in_specs=[vmem, vmem, anywhere],
        out_specs=(vmem,) + (anywhere,) * 6,
        scratch_shapes=[
            pltpu.VMEM((PL, ROWS, COLS), i32),
            pltpu.VMEM((PL * ROWS, COLS), f32),
            pltpu.VMEM((PL * ROWS, COLS), f32),
            pltpu.VMEM((2, PH, PL, ROWS, 128), bf16),
            pltpu.VMEM((4, 16, 128), bf16),
            pltpu.VMEM((4, 8, 128), i32),
            pltpu.VMEM((64, 64), f32),
            pltpu.VMEM((32, 64), f32),
            pltpu.VMEM((NX - 1, 32, 64), f32),
            pltpu.VMEM((NY - 1, 32, 64), f32),
            pltpu.VMEM((NZ - 1, 32, 64), f32),
            pltpu.VMEM((4, 32, 64), f32),
            pltpu.VMEM((64, 64), f32),
            pltpu.SemaphoreType.DMA((2,)),
            pltpu.SemaphoreType.DMA((2 * sum(SHARE) + 12,)),
            pltpu.SemaphoreType.DMA((2 * sum(SHARE) + 12,)),
            pltpu.SemaphoreType.DMA((sums,)),
            pltpu.SemaphoreType.DMA((sums,)),
        ],
        compiler_params=pltpu.CompilerParams(collective_id=0, has_side_effects=True),
        name="histogram_and_halo",
    )(bins, mask, atlas)


def fit(table, mean, scale):
    wide = [jnp.broadcast_to(table[r : r + 1, :], (PH, 128)) for r in range(NB // 128)]
    counts = jnp.concatenate(wide, axis=1)
    at = lax.broadcasted_iota(jnp.int32, (PH, NB), 1)
    bins = 64 * (at // 128) + (at & 63) + NB // 128 * (at & 64)
    centers = (bins.astype(jnp.float32) + 0.5) / NB
    first_w = counts * centers
    second_w = first_w * centers
    var = scale * scale
    weight = jnp.full((PH, 1), 1.0 / PH, jnp.float32)
    for step in range(EM_ITERS):
        diff = centers - mean
        scores = (jnp.log(weight) - 0.5 * jnp.log(var)) - diff * diff * (0.5 / var)
        e = jnp.exp(scores - jnp.max(scores, axis=0, keepdims=True))
        resp = e * (1.0 / jnp.sum(e, axis=0, keepdims=True))
        occ = jnp.sum(resp * counts, axis=1, keepdims=True)
        first = jnp.sum(resp * first_w, axis=1, keepdims=True)
        second = jnp.sum(resp * second_w, axis=1, keepdims=True)
        mean = first / (occ + 1.0)
        var = (second - first * mean) / (occ + 1.0) + VAR_EPS
        weight = (occ + 1.0) / (jnp.sum(occ, axis=0, keepdims=True) + float(PH))
    return mean, var, weight


def total_of(parts, op):
    while len(parts) > 1:
        parts = [op(a, b) for a, b in zip(parts[::2], parts[1::2])]
    return parts[0]


def softmax_into(t, mask):
    e = [jnp.exp2(v) for v in t]
    inv = mask / total_of(e, jnp.add)
    return [v * inv for v in e]


def back_kernel(
    counts_ref, mean_ref, scale_ref, bins_ref, mask_ref, atlas_ref,
    rows_a, side_a, corner_a, rows_c, side_c, corner_c, w_ref,
    prob_ref, params_ref, density_ref,
    table, apad, cpad, coef, uns, msk, held, held24, pa, pb, pd, across, kept,
):
    f32, bf16 = jnp.float32, jnp.bfloat16
    gy, gx = lax.axis_index("gy"), lax.axis_index("gx")
    ny, nx = lax.axis_size("gy"), lax.axis_size("gx")

    table[...] = jnp.concatenate([counts_ref[0:32, :], counts_ref[32:64, :]], axis=1)
    start = 2 * gy + gx // 4
    row = table[pl.ds(lax.rem(start, 32), 1), :] * place_scale(bins_ref)
    skip = start // 32 * 64 + lax.rem(gx, 4) * 16
    density_ref[...] = pltpu.roll(jnp.broadcast_to(row, (8, 128)), lax.rem(128 - skip, 128), 1)[0:1, 0:16]
    phase = lax.broadcasted_iota(jnp.int32, (PH, 1), 0)
    mean, scale = jnp.zeros((PH, 1), f32), jnp.zeros((PH, 1), f32)
    for k in range(PH):
        mean = jnp.where(phase == k, mean_ref[k], mean)
        scale = jnp.where(phase == k, scale_ref[k], scale)
    mean, var, weight = fit(table, mean, scale)
    lane = lax.broadcasted_iota(jnp.int32, (PH, 128), 1)
    diag = lane == lax.broadcasted_iota(jnp.int32, (PH, 128), 0)
    for n, column in enumerate((mean, var, weight)):
        spread = jnp.where(diag, jnp.broadcast_to(column, (PH, 128)), 0.0)
        params_ref[n : n + 1, :] = jnp.sum(spread, axis=0, keepdims=True)[:, 0:PH]
    offset = (jnp.log(weight) - 0.5 * jnp.log(var)) * LOG2E
    slope = (0.5 * LOG2E) / var
    for n, column in enumerate((mean, offset, slope)):
        full = jnp.broadcast_to(column, (PH, 128))
        for k in range(PH):
            coef[n, k] = jnp.broadcast_to(full[k : k + 1, :], (8, 128))

    own, over = pl.ds(128, COLS), pl.ds(128 + COLS, 128)

    def fill(k, carry):
        for plane in range(PL):
            apad[k, plane, 8:24, own] = atlas_ref[k, plane]
            apad[k, plane, 8:24, 0:128] = side_a[0, k, plane]
            apad[k, plane, 8:24, over] = side_a[1, k, plane]
            apad[k, plane, 8 - HALO : 8, own] = rows_a[0, k, plane]
            apad[k, plane, 24 : 24 + HALO, own] = rows_a[1, k, plane]
        return carry

    lax.fori_loop(0, PH, fill, 0)
    corners = [corner_a[n].astype(f32) for n in range(4)]
    for n in range(4):
        rows, lanes = pl.ds(24 * (n // 2), 8), (pl.ds(0, 128), over)[n % 2]
        for k in range(PH):
            for plane in range(PL):
                tile, i = divmod(k * PL + plane, 16)
                v = corners[n][8 * tile : 8 * tile + 8]
                v = pltpu.roll(v, (120 * (1 - n % 2) + 128 - 8 * i) % 128, 1)
                apad[k, plane, rows, lanes] = v.astype(bf16)
    has_up, has_down = gy > 0, gy < ny - 1
    has_left, has_right = gx > 0, gx < nx - 1
    cpad[:, 8:24, own] = bins_ref[...] + NB * mask_ref[...]
    cpad[:, 8:24, 0:128] = jnp.where(has_left, side_c[0], 0)
    cpad[:, 8:24, over] = jnp.where(has_right, side_c[1], 0)
    cpad[:, 8 - HALO : 8, own] = jnp.where(has_up, rows_c[0], 0)
    cpad[:, 24 : 24 + HALO, own] = jnp.where(has_down, rows_c[1], 0)
    for n in range(4):
        valid = (has_up, has_down)[n // 2] & (has_left, has_right)[n % 2]
        rows, lanes = pl.ds(24 * (n // 2), 8), (pl.ds(0, 128), over)[n % 2]
        for plane in range(PL):
            v = pltpu.roll(corner_c[n], (120 * (1 - n % 2) + 128 - 8 * plane) % 128, 1)
            cpad[plane, rows, lanes] = jnp.where(valid, v, 0)
    for ref in (pa, pb, pd):
        for plane in range(PL):
            ref[plane, 0:8] = jnp.zeros((8, 128), f32)
            ref[plane, 200:208] = jnp.zeros((8, 128), f32)
    beta = BETA / 5.0 * LOG2E
    at = lax.broadcasted_iota(jnp.int32, (8, 128), 1)

    def spread_sums(src, per, lead, pair):
        both = jnp.concatenate([src[2 * pair], src[2 * pair + 1]], axis=1)
        out = jnp.dot(both, w_ref[...], preferred_element_type=f32)
        span = pl.ds(lead, per)
        for i in range(2):
            for n, ref in enumerate((pa, pb, pd)):
                m = 3 * i + n
                ref[2 * pair + i, span, :] = out[:, 128 * m : 128 * m + 128]

    def update(side, plane, start, u_start, m_start, per):
        t = []
        for k in range(PH):
            r = k * per + start
            total = pa[plane, pl.ds(r, 8), :]
            if plane in (1, 2):
                total = total + across[side, 2 - plane, pl.ds(r, 8), :]
            total = total + (pb[plane, pl.ds(r - 1, 8), :] + pb[plane, pl.ds(r + 1, 8), :])
            total = total + (pd[plane, pl.ds(r - 2, 8), :] + pd[plane, pl.ds(r + 2, 8), :])
            t.append(uns[plane, pl.ds(k * 32 + u_start, 8), :] + beta * total)
        return softmax_into(t, msk[plane, pl.ds(m_start, 8), :])

    def store(side, ref, plane, row, lead, both):
        both = both.astype(bf16)
        ref[plane, pl.ds(row, 16), :] = both
        if plane in (1, 2):
            across[side, plane - 1, pl.ds(row + lead, 16), :] = 5.0 * both.astype(f32)

    def chunk(c, carry):
        turn = 12 * c + 6
        from_right = at < 128 - turn

        def moved(a, b):
            return pltpu.roll(jnp.where(from_right, b, a), turn, 1)

        tile_a = pl.ds(pl.multiple_of(c * 128, 128), 128)
        tile_b = pl.ds(pl.multiple_of((c + 1) * 128, 128), 128)
        wide_right = jnp.concatenate([from_right, from_right], axis=0)

        def begin(plane):
            for pair in range(2):
                outs = []
                rows16 = pl.ds(pair * 16, 16)
                prior = []
                for k in range(PH):
                    one = apad[k, plane, rows16, tile_a].astype(f32)
                    two = apad[k, plane, rows16, tile_b].astype(f32)
                    prior.append(jnp.where(wide_right, two, one))
                for sub in range(2):
                    g = pair * 16 + sub * 8
                    s8 = slice(sub * 8, sub * 8 + 8)
                    cd = moved(cpad[plane, pl.ds(g, 8), tile_a], cpad[plane, pl.ds(g, 8), tile_b])
                    keep = cd >= NB
                    m = jnp.where(keep, 1.0, 0.0)
                    msk[plane, pl.ds(g, 8), :] = m
                    s = ((cd & (NB - 1)).astype(f32) + 0.5) * (1.0 / NB)
                    t = []
                    for k in range(PH):
                        d = s - coef[0, k]
                        u = (coef[1, k] - d * d * coef[2, k]) + pltpu.roll(prior[k][s8], turn, 1) * LOG2E
                        t.append(u)
                    top = total_of(t, jnp.maximum)
                    t = [u - top for u in t]
                    for k in range(PH):
                        uns[plane, pl.ds(k * 32 + g, 8), :] = t[k]
                    outs.append(softmax_into(t, m))
                for k in range(PH):
                    store(0, held, plane, k * 32 + pair * 16, 0, jnp.concatenate([outs[0][k], outs[1][k]], axis=0))

        def store24(side, plane, outs):
            flat = [outs[i][k] for k in range(PH) for i in range(3)]
            for f in range(0, 3 * PH, 2):
                store(side, held24, plane, f * 8, 8, jnp.concatenate([flat[f], flat[f + 1]], axis=0))

        for plane in range(PL):
            begin(plane)
        for pair in range(PL // 2):
            spread_sums(held, 256, 0, pair)
        for plane in range(PL):
            store24(1, plane, [update(0, plane, 4 + 8 * i, 4 + 8 * i, 4 + 8 * i, 32) for i in range(3)])
        for pair in range(PL // 2):
            spread_sums(held24, 192, 8, pair)
        for plane in range(PL):
            store24(0, plane, [update(1, plane, 8 + 8 * i, 4 + 8 * i, 4 + 8 * i, 24) for i in range(3)])
        for pair in range(PL // 2):
            spread_sums(held24, 192, 8, pair)
        slot = lax.rem(c, 2)
        before = at < STEP + 12 - 12 * c
        tile_out = pl.ds(pl.multiple_of(jnp.maximum(c - 1, 0) * 128, 128), 128)
        for plane in range(PL):
            outs = [update(0, plane, 8 + 4 + 8 * i, 8 + 8 * i, 8 + 8 * i, 24) for i in range(2)]
            for k in range(PH):
                full = []
                for i in range(2):
                    v = pltpu.roll(outs[i][k], 128 - turn, 1)
                    old = kept[1 - slot, plane, k, pl.ds(8 * i, 8), :]
                    kept[slot, plane, k, pl.ds(8 * i, 8), :] = v
                    full.append(jnp.where(before, old, v))
                prob_ref[k, plane, :, tile_out] = jnp.concatenate(full, axis=0).astype(bf16)
        return carry

    lax.fori_loop(0, CHUNKS, chunk, 0)


def place_scale(bins_ref):
    planes, rows, cols = bins_ref.shape
    return float(NB) / float(planes * rows * cols * 2 * NX * NY * NZ)


def stencil_weights():
    i = np.arange(128)
    d = np.abs(i[:, None] - i[None, :])

    def band(*values):
        out = np.zeros((128, 128), np.float32)
        for n, v in enumerate(values):
            out[d == n] = v
        return out

    flat, one, two = band(0.0, 5.0, 1.25), band(5.0, 2.5, 1.0), band(1.25, 1.0, 0.625)
    eye, none = band(5.0), np.zeros((128, 128), np.float32)
    upper = np.concatenate([flat, one, two, eye, none, none], 1)
    lower = np.concatenate([eye, none, none, flat, one, two], 1)
    return np.concatenate([upper, lower], 0)


def back(counts, mean, scale, bins, mask, atlas, halos):
    f32, bf16, i32 = jnp.float32, jnp.bfloat16, jnp.int32
    vmem, smem = pl.BlockSpec(memory_space=pltpu.VMEM), pl.BlockSpec(memory_space=pltpu.SMEM)
    sds = jax.ShapeDtypeStruct
    weights = jnp.asarray(stencil_weights(), bf16)
    return pl.pallas_call(
        back_kernel,
        out_shape=(sds((PH, PL, ROWS, COLS), bf16), sds((3, PH), f32), sds((1, 16), f32)),
        in_specs=[vmem, smem, smem] + [vmem] * 10,
        out_specs=(vmem, vmem, vmem),
        scratch_shapes=[
            pltpu.VMEM((NB // 128, 128), f32),
            pltpu.VMEM((PH, PL, 32, COLS + 256), bf16),
            pltpu.VMEM((PL, 32, COLS + 256), i32),
            pltpu.VMEM((3, PH, 8, 128), f32),
            pltpu.VMEM((PL, PH * 32, 128), f32),
            pltpu.VMEM((PL, 32, 128), f32),
            pltpu.VMEM((PL, PH * 32, 128), bf16),
            pltpu.VMEM((PL, PH * 24, 128), bf16),
            pltpu.VMEM((PL, PH * 32, 128), f32),
            pltpu.VMEM((PL, PH * 32, 128), f32),
            pltpu.VMEM((PL, PH * 32, 128), f32),
            pltpu.VMEM((2, 2, PH * 32, 128), f32),
            pltpu.VMEM((2, PL, PH, ROWS, 128), f32),
        ],
        name="fit_and_label",
    )(counts, mean, scale, bins, mask, atlas, *halos, weights)


def per_device(bins, mask, atlas, init_mean, init_scale):
    counts, *halos = front(bins, mask, atlas)
    prob, params, density = back(counts, init_mean, init_scale, bins, mask, atlas, halos)
    return prob, params, density.reshape(-1)


def solution(mesh):
    in_specs = (P(None, "gy", "gx"), P(None, "gy", "gx"), P(None, None, "gy", "gx"), P(), P())
    out_specs = (P(None, None, "gy", "gx"), P(), P(("gy", "gx")))
    return jax.shard_map(
        per_device, mesh=mesh, in_specs=in_specs, out_specs=out_specs, check_vma=False
    )
```
